256 devices in a mesh: seq: 4 (over z_lo), row: 16 (over x, z_hi, core), col: 4 (over y).
Axes of the slice: x: 4, y: 4, z: 8 (z_hi: 2, z_lo: 4; z = z_hi * 4 + z_lo), core: 2. Of those that a mesh axis runs over, the one named last changes fastest.
Arguments:
- grads: bfloat16 [1024, 28672], P('row', ('seq', 'col')), may hold values from -6 to 6
- acts: bfloat16 [1024, 8192], P(('seq', 'col'), 'row'), may hold values from -6 to 6
- out_basis: bfloat16 [28672, 28672], P(('seq', 'col'), 'row'), may hold values from -0.03125 to 0.03125
- in_basis: bfloat16 [8192, 8192], P('row', ('seq', 'col')), may hold values from -0.0625 to 0.0625
- lengths: int32 [4], replicated, may hold values from 1 to 256, 768 in all
Outputs:
- eigenvalues: float32 [28672, 8192], P('row', ('seq', 'col'))
The draws below stay inside these ranges and needn't reach their ends.
Inputs may be any that keep to these rules, and one draw needn't show every extreme that they name: lengths sum to 768; some sequence is full.
All inputs are finite; a program needn't handle non-finite values.
Results may differ from the reference program's by a relative error of at most 0.0036.
Values may be sent and summed in bfloat16 or wider, within the bound.
A program may use at most 64 MiB of HBM per device.

```python
import math
import jax
import jax.numpy as jnp
import numpy as np
from jax import lax

DIN = 8192
DOUT = 28672
SEQ_LEN = 256
SEQS = 4
TOKENS = 1024


def level_of(stream_key, shape, split, least, high):
    factor_of, own = 1.0, jax.random.fold_in(stream_key, 6)
    for dim, shards_of in split:
        steps = jnp.exp(jax.random.uniform(jax.random.fold_in(own, dim), (shards_of,), jnp.float32, least / len(split), high / len(split)))
        factor_of = factor_of * jnp.repeat(steps, shape[dim] // shards_of).reshape([-1 if axis == dim else 1 for axis in range(len(shape))])
    return factor_of


def profile(count, total, reach, slope):
    portions = [(1 << 20) // math.isqrt(standing ** slope) + 1 for standing in range(2, count + 1)]
    surplus, counts = total - reach - (count - 1), [1] * (count - 1)
    while surplus > 0:
        free = [i for i in range(count - 1) if counts[i] < reach]
        pool, budget = sum([portions[i] for i in free]), surplus
        for i in free:
            addition = min(reach - counts[i], max(1, budget * portions[i] // pool), surplus)
            counts[i] = counts[i] + addition
            surplus = surplus - addition
    return np.array([reach] + counts)


def ragged(key, count, total, reach, skew):
    if count == 2:
        one = jax.random.randint(key, (), max(1, total - reach), min(reach, total - 1) + 1)
        return jnp.stack([one, total - one])
    tallies = jnp.asarray(profile(count, total, reach, skew), jnp.int32)
    couples = (count - 1) // 2
    donor, receiver = tallies[1:1 + 2 * couples:2], tallies[2:2 + 2 * couples:2]
    room = jnp.minimum(donor - 1, reach - receiver)
    shifted = jax.random.randint(jax.random.fold_in(key, 1), (couples,), 0, 1 << 20) % (room + 1)
    tallies = tallies.at[1:1 + 2 * couples:2].set(donor - shifted).at[2:2 + 2 * couples:2].set(receiver + shifted)
    return tallies[jax.random.permutation(jax.random.fold_in(key, 2), count)]


def centred(stream_key, dims, scale, most, cuts=(), held_as=jnp.bfloat16):
    result = jax.random.normal(stream_key, dims, jnp.float32) * scale
    if len(cuts) > 0:
        result = level_of(stream_key, dims, cuts, -0.22, 0.18) * result
    return jnp.clip(result, min=-most, max=most).astype(held_as)


def setup_inputs(seed: int = 0) -> dict:
    key_list = jax.random.split(jax.random.key(seed), 6)
    grads = centred(key_list[0], (TOKENS, DOUT), 1.0, 6.0, ((0, 16), (1, 16)))
    acts = centred(key_list[1], (TOKENS, DIN), 1.0, 6.0, ((0, 16), (1, 16)))
    out_basis = centred(key_list[2], (DOUT, DOUT), DOUT ** -0.5, 0.03125, ((0, 16), (1, 16)))
    in_basis = centred(key_list[3], (DIN, DIN), DIN ** -0.5, 0.0625, ((0, 16), (1, 16)))
    lengths = ragged(key_list[4], SEQS, 3 * SEQ_LEN, SEQ_LEN, 2).astype(jnp.int32)
    return dict(grads=grads, acts=acts, out_basis=out_basis, in_basis=in_basis, lengths=lengths)


def reference(grads, acts, out_basis, in_basis, lengths):
    grad_proj = jnp.dot(grads, out_basis, preferred_element_type=jnp.float32).astype(jnp.bfloat16)
    act_full = jnp.dot(acts, in_basis, preferred_element_type=jnp.float32)
    token_index = jnp.arange(TOKENS, dtype=jnp.int32)
    seq_owner = token_index // SEQ_LEN
    position = token_index % SEQ_LEN
    is_live = (position < lengths[seq_owner]).astype(jnp.float32)
    act_proj = (act_full * is_live[:, None]).astype(jnp.bfloat16)
    grad_three = grad_proj.reshape(SEQS, SEQ_LEN, DOUT)
    act_three = act_proj.reshape(SEQS, SEQ_LEN, DIN)

    def accumulate(total, pair):
        grad_seq = lax.dot_general(pair[0], pair[1], (((0,), (0,)), ((), ())), preferred_element_type=jnp.float32)
        return total + grad_seq * grad_seq, None

    total, unused = lax.scan(accumulate, jnp.zeros((DOUT, DIN), jnp.float32), (grad_three, act_three))
    return total / (SEQS * SEQ_LEN)
```

```python
import functools

import jax
import jax.numpy as jnp
from jax import lax
from jax.experimental import pallas as pl
from jax.experimental.pallas import tpu as pltpu
from jax.sharding import PartitionSpec as P

SEQ = 256
LIVE = 768
PIECE = 48
COLS = 256
MESH = pl.DeviceIdType.MESH
F32, BF16 = jnp.float32, jnp.bfloat16


def kernel(
    chunks,
    len_ref, grads_ref, acts_ref, ob_ref, ib_ref, out_ref,
    xg, xa, ob, ib, gc, ac,
    pf, y1s, y1r, y2s, y2r, zs, zr, gp,
    pa, kr, x1r, x2r, hr, ap, am, gt, ob_out,
    loc, out_sem, g_s, g_r, a_s, a_r, p_s, p_r, c_s, c_r,
):
    s, r, c = lax.axis_index("seq"), lax.axis_index("row"), lax.axis_index("col")
    core, half, x = r % 2, (r // 2) % 2, r // 4
    xp, xm, x2 = (x + 1) % 4, (x + 3) % 4, (x + 2) % 4
    cp, cm, c2 = (c + 1) % 4, (c + 3) % 4, (c + 2) % 4

    def row_of(x_at, half_at, core_at):
        return x_at * 4 + half_at * 2 + core_at

    to_core = {"row": row_of(x, half, 1 - core)}
    to_half = {"row": row_of(x, 1 - half, core)}
    to_xp, to_xm = {"row": row_of(xp, half, core)}, {"row": row_of(xm, half, core)}
    to_cp, to_cm = {"col": cp}, {"col": cm}
    to_seq = [{"seq": (s + d) % 4} for d in (1, 2, 3)]

    def remote(src, dst, send, recv, to):
        return pltpu.make_async_remote_copy(
            src_ref=src, dst_ref=dst, send_sem=send, recv_sem=recv, device_id=to, device_id_type=MESH
        )

    load_g = pltpu.make_async_copy(grads_ref, xg.at[r], loc.at[0])
    load_a = pltpu.make_async_copy(acts_ref, xa.at[c, s], loc.at[1])
    load_ib = pltpu.make_async_copy(ib_ref, ib, loc.at[2])
    load_ob = pltpu.make_async_copy(ob_ref, ob, loc.at[3])
    load_g.start()
    load_a.start()

    barrier = pltpu.get_barrier_semaphore()
    for to in (to_core, to_half, to_xp, to_xm, to_cp, to_cm, *to_seq):
        pl.semaphore_signal(barrier, inc=1, device_id=to, device_id_type=MESH)
    load_g.wait()
    load_a.wait()
    pl.semaphore_wait(barrier, 9)

    def block(x_at, half_at, core_at):
        return xg.at[row_of(x_at, half_at, core_at)]

    mine, other = block(x, half, core), block(x, 1 - half, core)
    n_send = [0]
    sends = []

    def send_g(src, recv, to):
        cp_ = remote(src, src, g_s.at[n_send[0]], g_r.at[recv], to)
        n_send[0] += 1
        cp_.start()
        sends.append(cp_)

    def got_g(dst, recv):
        remote(dst, dst, g_s.at[0], g_r.at[recv], to_core).wait_recv()

    send_g(mine.at[0], 2, to_xp)
    send_g(mine.at[1], 5, to_xm)
    send_g(mine.at[0], 0, to_half)
    send_g(mine.at[1], 1, to_half)
    send_g(mine.at[1], 3, to_xp)
    send_g(mine.at[0], 4, to_xm)
    send_g(mine, 14, to_core)

    a_sends = []

    def send_a(src, i, to):
        cp_ = remote(src, src, a_s.at[i], a_r.at[i], to)
        cp_.start()
        a_sends.append(cp_)

    def got_a(dst, i):
        remote(dst, dst, a_s.at[i], a_r.at[i], to_core).wait_recv()

    for d in range(3):
        send_a(xa.at[c, s], d, to_seq[d])
    load_ib.start()
    load_ob.start()

    got_g(block(xm, half, core).at[0], 2)
    send_g(block(xm, half, core).at[0], 6, to_xp)
    got_g(block(xp, half, core).at[1], 5)
    send_g(block(xp, half, core).at[1], 7, to_xm)

    for d in range(3):
        got_a(xa.at[c, (s + 3 - d) % 4], d)
    send_a(xa.at[c], 3, to_cp)
    send_a(xa.at[c], 4, to_cm)

    got_g(other.at[0], 0)
    send_g(other.at[0], 8, to_xp)
    send_g(other.at[0], 10, to_xm)
    got_g(block(xm, half, core).at[1], 3)
    send_g(block(xm, half, core), 15, to_core)
    got_g(block(xp, half, core).at[0], 4)
    send_g(block(xp, half, core), 16, to_core)
    got_g(other.at[1], 1)
    send_g(other.at[1], 11, to_xm)
    send_g(other.at[1], 9, to_xp)
    send_g(other, 17, to_core)
    got_g(block(x2, half, core).at[0], 6)
    got_g(block(x2, half, core).at[1], 7)
    send_g(block(x2, half, core), 18, to_core)

    got_a(xa.at[cm], 3)
    send_a(xa.at[cm, 0:2], 5, to_cp)
    got_a(xa.at[cp], 4)
    send_a(xa.at[cp, 2:4], 6, to_cm)

    got_g(block(xm, 1 - half, core).at[0], 8)
    send_g(block(xm, 1 - half, core).at[0], 12, to_xp)
    got_g(block(xp, 1 - half, core).at[1], 11)
    send_g(block(xp, 1 - half, core).at[1], 13, to_xm)

    lens = [len_ref[q] for q in range(4)]
    offs = [jnp.int32(0)]
    for q in range(3):
        offs.append(offs[-1] + lens[q])

    def pick(i):
        rows = lax.broadcasted_iota(jnp.int32, (SEQ, SEQ), 0) + i * SEQ
        slot = lax.broadcasted_iota(jnp.int32, (SEQ, SEQ), 1)
        tiles = []
        for q in (i, i + 1):
            hit = jnp.logical_and(rows == slot + offs[q], slot < lens[q])
            tiles.append(jnp.where(hit, 1.0, 0.0).astype(BF16))
        return jnp.concatenate(tiles, axis=1)

    got_a(xa.at[c2, 0:2], 5)
    got_a(xa.at[c2, 2:4], 6)
    load_ib.wait()
    for i in range(3):
        rows = jnp.concatenate([xa[b, q] for q in (i, i + 1) for b in range(4)], axis=0)
        packed = jnp.dot(pick(i), rows, preferred_element_type=F32)
        ac[i * SEQ : (i + 1) * SEQ, :] = packed.astype(BF16)
    pa[...] = jnp.dot(ac[...], ib[...], preferred_element_type=F32).reshape(pa.shape)

    p_sends = []

    def send_p(src, dst, i, to):
        cp_ = remote(src, dst, p_s.at[i], p_r.at[i], to)
        cp_.start()
        return cp_

    def got_p(dst, i):
        remote(dst, dst, p_s.at[i], p_r.at[i], to_core).wait_recv()

    send_p(pa.at[1 - core], kr, 0, to_core)

    got_g(block(xm, 1 - half, core).at[1], 9)
    send_g(block(xm, 1 - half, core), 19, to_core)
    got_g(block(xp, 1 - half, core).at[0], 10)
    send_g(block(xp, 1 - half, core), 20, to_core)
    got_g(block(x2, 1 - half, core).at[0], 12)
    got_g(block(x2, 1 - half, core).at[1], 13)
    send_g(block(x2, 1 - half, core), 21, to_core)
    for n, (x_at, half_at) in enumerate(
        ((x, half), (xm, half), (xp, half), (x, 1 - half), (x2, half), (xm, 1 - half), (xp, 1 - half), (x2, 1 - half))
    ):
        got_g(block(x_at, half_at, 1 - core), 14 + n)

    for i in range(3):
        chosen = pick(i)

        def packed_columns(j, carry, i=i, chosen=chosen):
            cols = pl.ds(pl.multiple_of(j * COLS, COLS), COLS)
            rows = xg[4 * i : 4 * i + 8, :, :, cols].reshape(2 * SEQ, COLS)
            packed = jnp.dot(chosen, rows, preferred_element_type=F32)
            gc[i * SEQ : (i + 1) * SEQ, cols] = packed.astype(BF16)
            return carry

        lax.fori_loop(0, chunks, packed_columns, 0)
    load_ob.wait()

    def c_copy(src, dst, i, n, to):
        return remote(src, dst, c_s.at[i, n], c_r.at[i, n], to)

    def multiply(i):
        cols = pl.ds(pl.multiple_of(i * COLS, COLS), COLS)
        pf[i] = jnp.dot(gc[...], ob[:, cols], preferred_element_type=F32).reshape(pf.shape[1:])
        y1s[i] = pf[i, c2].astype(BF16)

    def y1_copies(i):
        return (
            c_copy(y1s.at[i, 0:2], y1r.at[i, 0], i, 0, to_cp),
            c_copy(y1s.at[i, 2:4], y1r.at[i, 1], i, 1, to_cm),
        )

    def y2_copies(i):
        return (
            c_copy(y2s.at[i, 0], y2r.at[i, 0], i, 2, to_cp),
            c_copy(y2s.at[i, 1], y2r.at[i, 1], i, 3, to_cm),
        )

    def z_copies(i):
        return tuple(
            c_copy(zs.at[i, (s + d) % 4], zr.at[i, d - 1], i, 3 + d, to_seq[d - 1]) for d in (1, 2, 3)
        )

    def za_copies(i):
        return tuple(c_copy(gp.at[i, c, s], gp.at[i, c, s], i, 6 + d, to_seq[d - 1]) for d in (1, 2, 3))

    def ya1_copies(i):
        return (
            c_copy(gp.at[i, c], gp.at[i, c], i, 10, to_cp),
            c_copy(gp.at[i, c], gp.at[i, c], i, 11, to_cm),
        )

    def ya2_copies(i):
        return (
            c_copy(gp.at[i, cm, 0:2], gp.at[i, cm, 0:2], i, 12, to_cp),
            c_copy(gp.at[i, cp, 2:4], gp.at[i, cp, 2:4], i, 13, to_cm),
        )

    def start(copies):
        for copy in copies:
            copy.start()

    def arrived(copies):
        for copy in copies:
            copy.wait_recv()

    def out_copy(i):
        rows = pl.ds(pl.multiple_of(i * COLS, COLS), COLS)
        return pltpu.make_async_copy(ob_out.at[i], out_ref.at[rows], out_sem.at[i])

    def step(t, carry):
        @pl.when(t < chunks)
        def _():
            multiply(t)
            start(y1_copies(t))

        @pl.when(jnp.logical_and(t >= 1, t < chunks + 1))
        def _():
            i = t - 1
            arrived(y1_copies(i))
            y2s[i, 0, 0:2] = (pf[i, cp, 0:2] + y1r[i, 0].astype(F32)).astype(BF16)
            y2s[i, 0, 2:4] = pf[i, cp, 2:4].astype(BF16)
            y2s[i, 1, 0:2] = pf[i, cm, 0:2].astype(BF16)
            y2s[i, 1, 2:4] = (pf[i, cm, 2:4] + y1r[i, 1].astype(F32)).astype(BF16)
            start(y2_copies(i))

        @pl.when(jnp.logical_and(t >= 2, t < chunks + 2))
        def _():
            i = t - 2
            arrived(y2_copies(i))
            total = pf[i, c] + y2r[i, 0].astype(F32) + y2r[i, 1].astype(F32)
            pf[i, c] = total
            zs[i] = total.astype(BF16)
            start(z_copies(i))

        @pl.when(jnp.logical_and(t >= 3, t < chunks + 3))
        def _():
            i = t - 3
            arrived(z_copies(i))
            total = pf[i, c, s]
            for d in range(3):
                total = total + zr[i, d].astype(F32)
            gp[i, c, s] = total.astype(BF16)
            start(za_copies(i))

        @pl.when(jnp.logical_and(t >= 4, t < chunks + 4))
        def _():
            i = t - 4
            for d in range(3):
                piece = gp.at[i, c, (s + 3 - d) % 4]
                c_copy(piece, piece, i, 7 + d, to_core).wait_recv()
            start(ya1_copies(i))

        @pl.when(jnp.logical_and(t >= 5, t < chunks + 5))
        def _():
            i = t - 5
            c_copy(gp.at[i, cm], gp.at[i, cm], i, 10, to_core).wait_recv()
            c_copy(gp.at[i, cp], gp.at[i, cp], i, 11, to_core).wait_recv()
            start(ya2_copies(i))

        @pl.when(t == 0)
        def _():
            got_p(kr, 0)
            pa[core] = pa[core] + kr[...]
            send_p(pa.at[core, x2, 0], x1r.at[0], 1, to_xp)
            send_p(pa.at[core, x2, 1], x1r.at[1], 2, to_xm)

        @pl.when(t == 1)
        def _():
            got_p(x1r.at[0], 1)
            got_p(x1r.at[1], 2)
            pa[core, xp, 0] = pa[core, xp, 0] + x1r[0]
            pa[core, xm, 1] = pa[core, xm, 1] + x1r[1]
            send_p(pa.at[core, xp], x2r.at[0], 3, to_xp)
            send_p(pa.at[core, xm], x2r.at[1], 4, to_xm)

        @pl.when(t == 2)
        def _():
            got_p(x2r.at[0], 3)
            got_p(x2r.at[1], 4)
            pa[core, x] = pa[core, x] + x2r[0] + x2r[1]
            send_p(pa.at[core, x, 1 - half], hr, 5, to_half)

        @pl.when(t == 3)
        def _():
            got_p(hr, 5)
            ap[core, x, half] = (pa[core, x, half] + hr[...]).astype(BF16)
            send_p(ap.at[core, x, half], ap.at[core, x, half], 6, to_half)

        @pl.when(t == 4)
        def _():
            got_p(ap.at[core, x, 1 - half], 6)
            send_p(ap.at[core, x], ap.at[core, x], 7, to_xp)
            send_p(ap.at[core, x], ap.at[core, x], 8, to_xm)

        @pl.when(t == 5)
        def _():
            got_p(ap.at[core, xm], 7)
            got_p(ap.at[core, xp], 8)
            send_p(ap.at[core, xm, 0], ap.at[core, xm, 0], 9, to_xp)
            send_p(ap.at[core, xp, 1], ap.at[core, xp, 1], 10, to_xm)

        @pl.when(t == 6)
        def _():
            got_p(ap.at[core, x2, 0], 9)
            got_p(ap.at[core, x2, 1], 10)
            send_p(ap.at[core], ap.at[core], 11, to_core)

        @pl.when(t == 7)
        def _():
            got_p(ap.at[1 - core], 11)
            place = 0
            for q, (low, high) in enumerate(((0, 1), (0, 2), (1, 3), (2, 3))):
                for b in range(low, high):
                    rows = lax.broadcasted_iota(jnp.int32, (SEQ, ap.shape[-1]), 0) + b * SEQ
                    inside = jnp.logical_and(rows >= offs[q], rows < offs[q] + lens[q])
                    share = ap[...].reshape(LIVE, ap.shape[-1])[b * SEQ : (b + 1) * SEQ]
                    am[place : place + SEQ, :] = jnp.where(inside, share.astype(F32), 0.0).astype(BF16)
                    place += SEQ

        @pl.when(t >= 7)
        def _():
            i = t - 7
            c_copy(gp.at[i, c2, 0:2], gp.at[i, c2, 0:2], i, 12, to_core).wait_recv()
            c_copy(gp.at[i, c2, 2:4], gp.at[i, c2, 2:4], i, 13, to_core).wait_recv()
            gt[...] = gp[i].reshape(LIVE, COLS).T
            total, place = None, 0
            for low, high in ((0, 1), (0, 2), (1, 3), (2, 3)):
                depth = (high - low) * SEQ
                one = jnp.dot(
                    gt[:, low * SEQ : high * SEQ], am[place : place + depth, :], preferred_element_type=F32
                )
                total = one * one if total is None else total + one * one
                place += depth
            ob_out[i] = total * (1.0 / (4 * SEQ))
            out_copy(i).start()

        return carry

    lax.fori_loop(0, chunks + 7, step, 0)

    for copy in sends:
        copy.wait_send()
    for copy in a_sends:
        copy.wait_send()
    remote(pa.at[1 - core], kr, p_s.at[0], p_r.at[0], to_core).wait_send()
    for i in (1, 2):
        remote(x1r.at[0], x1r.at[0], p_s.at[i], p_r.at[i], to_core).wait_send()
    for i in (3, 4):
        remote(x2r.at[0], x2r.at[0], p_s.at[i], p_r.at[i], to_core).wait_send()
    remote(hr, hr, p_s.at[5], p_r.at[5], to_core).wait_send()
    remote(ap.at[core, x, half], ap.at[core, x, half], p_s.at[6], p_r.at[6], to_half).wait_send()
    for i in (7, 8):
        remote(ap.at[core, x], ap.at[core, x], p_s.at[i], p_r.at[i], to_xp).wait_send()
    for i in (9, 10):
        remote(ap.at[core, x, 0], ap.at[core, x, 0], p_s.at[i], p_r.at[i], to_xp).wait_send()
    remote(ap.at[core], ap.at[core], p_s.at[11], p_r.at[11], to_core).wait_send()

    def finish(i, carry):
        for copies in (y1_copies, y2_copies, z_copies, za_copies, ya1_copies, ya2_copies):
            for copy in copies(i):
                copy.wait_send()
        out_copy(i).wait()
        return carry

    lax.fori_loop(0, chunks, finish, 0)


def body(grads, acts, out_basis, in_basis, lengths):
    n_row, n_seq, n_col = lax.axis_size("row"), lax.axis_size("seq"), lax.axis_size("col")
    tokens, width = grads.shape
    a_width = acts.shape[1]
    directions, a_directions = out_basis.shape[1], in_basis.shape[1]
    chunks = directions // COLS
    piece = (PIECE, COLS)
    dma = pltpu.SemaphoreType.DMA
    return pl.pallas_call(
        functools.partial(kernel, chunks),
        out_shape=jax.ShapeDtypeStruct((directions, a_directions), F32),
        in_specs=[pl.BlockSpec(memory_space=pltpu.SMEM)] + [pl.BlockSpec(memory_space=pl.ANY)] * 4,
        out_specs=pl.BlockSpec(memory_space=pl.ANY),
        scratch_shapes=[
            pltpu.VMEM((n_row, 2, tokens // 2, width), BF16),
            pltpu.VMEM((n_col, n_seq, tokens, a_width), BF16),
            pltpu.VMEM(out_basis.shape, BF16),
            pltpu.VMEM(in_basis.shape, BF16),
            pltpu.VMEM((LIVE, width), BF16),
            pltpu.VMEM((LIVE, a_width), BF16),
            pltpu.VMEM((chunks, 4, 4, *piece), F32),
            pltpu.VMEM((chunks, 4, *piece), BF16),
            pltpu.VMEM((chunks, 2, 2, *piece), BF16),
            pltpu.VMEM((chunks, 2, 4, *piece), BF16),
            pltpu.VMEM((chunks, 2, 4, *piece), BF16),
            pltpu.VMEM((chunks, 4, *piece), BF16),
            pltpu.VMEM((chunks, 3, *piece), BF16),
            pltpu.VMEM((chunks, 4, 4, *piece), BF16),
            pltpu.VMEM((2, 4, 2, PIECE, a_directions), F32),
            pltpu.VMEM((4, 2, PIECE, a_directions), F32),
            pltpu.VMEM((2, PIECE, a_directions), F32),
            pltpu.VMEM((2, 2, PIECE, a_directions), F32),
            pltpu.VMEM((PIECE, a_directions), F32),
            pltpu.VMEM((2, 4, 2, PIECE, a_directions), BF16),
            pltpu.VMEM((6 * SEQ, a_directions), BF16),
            pltpu.VMEM((COLS, LIVE), BF16),
            pltpu.VMEM((chunks, COLS, a_directions), F32),
            dma((4,)),
            dma((chunks,)),
            dma((22,)),
            dma((22,)),
            dma((7,)),
            dma((7,)),
            dma((12,)),
            dma((12,)),
            dma((chunks, 14)),
            dma((chunks, 14)),
        ],
        compiler_params=pltpu.CompilerParams(
            collective_id=0, has_side_effects=True, vmem_limit_bytes=60 * 1024 * 1024
        ),
        name="eigen",
    )(lengths, grads.reshape(2, tokens // 2, width), acts, out_basis, in_basis)


def solution(mesh):
    in_specs = (
        P("row", ("seq", "col")),
        P(("seq", "col"), "row"),
        P(("seq", "col"), "row"),
        P("row", ("seq", "col")),
        P(),
    )
    out_specs = P("row", ("seq", "col"))
    return jax.shard_map(body, mesh=mesh, in_specs=in_specs, out_specs=out_specs, check_vma=False)
```

```python
import functools

import jax
import jax.numpy as jnp
from jax import lax
from jax.experimental import pallas as pl
from jax.experimental.pallas import tpu as pltpu
from jax.sharding import PartitionSpec as P

SEQ = 256
HALF = 128
LIVE = 768
PIECE = 48
COLS = 256
MESH = pl.DeviceIdType.MESH
F32, BF16 = jnp.float32, jnp.bfloat16


def kernel(
    chunks,
    len_ref, grads_ref, acts_ref, ob_ref, ib_ref, out_ref,
    xg, xa, ob, ib, gc, ac,
    pf0, y1s0, y1r0, y2s0, y2r0, zs0, zr0, gp0,
    pf1, y1s1, y1r1, y2s1, y2r1, zs1, zr1, gp1,
    pa, kr, x1r, x2r, hr, ap, am, gt, res,
    loc, out_sem, g_s, g_r, a_s, a_r, p_s, p_r, c_s0, c_r0, c_s1, c_r1,
):
    s, r, c = lax.axis_index("seq"), lax.axis_index("row"), lax.axis_index("col")
    core, half, x = r % 2, (r // 2) % 2, r // 4
    xp, xm, x2 = (x + 1) % 4, (x + 3) % 4, (x + 2) % 4
    cp, cm, c2 = (c + 1) % 4, (c + 3) % 4, (c + 2) % 4

    def row_of(x_at, half_at, core_at):
        return x_at * 4 + half_at * 2 + core_at

    to_core = {"row": row_of(x, half, 1 - core)}
    to_half = {"row": row_of(x, 1 - half, core)}
    to_xp, to_xm = {"row": row_of(xp, half, core)}, {"row": row_of(xm, half, core)}
    to_cp, to_cm = {"col": cp}, {"col": cm}
    to_seq = [{"seq": (s + d) % 4} for d in (1, 2, 3)]

    def remote(src, dst, send, recv, to):
        return pltpu.make_async_remote_copy(
            src_ref=src, dst_ref=dst, send_sem=send, recv_sem=recv, device_id=to, device_id_type=MESH
        )

    load_g = pltpu.make_async_copy(grads_ref, xg.at[x, half, core], loc.at[0])
    load_a = pltpu.make_async_copy(acts_ref, xa.at[c, s], loc.at[1])
    load_ib = pltpu.make_async_copy(ib_ref, ib, loc.at[2])
    load_ob = pltpu.make_async_copy(ob_ref, ob, loc.at[3])
    load_g.start()
    load_a.start()

    barrier = pltpu.get_barrier_semaphore()
    for to in (to_core, to_half, to_xp, to_xm, to_cp, to_cm, *to_seq):
        pl.semaphore_signal(barrier, inc=1, device_id=to, device_id_type=MESH)
    load_g.wait()
    load_a.wait()
    pl.semaphore_wait(barrier, 9)

    def block(x_at, half_at, core_at):
        return xg.at[x_at, half_at, core_at]

    mine, other = block(x, half, core), block(x, 1 - half, core)
    def send_g(src, recv, to, group=1):
        remote(src, src, g_s.at[group], g_r.at[recv], to).start()

    def to_partner(src, base):
        remote(src, src, g_s.at[2], g_r.at[14 + base], to_core).start()

    def got_g(dst, recv):
        remote(dst, dst, g_s.at[0], g_r.at[recv], to_core).wait_recv()

    def near(base):
        return block(xm, 1 - half if base else half, core)

    def far(base):
        return block(xp, 1 - half if base else half, core)

    def relay_low(base):
        got_g(near(base).at[0], 2 + 6 * base)
        send_g(near(base).at[0], 6 + 6 * base, to_xp)

    def relay_high(base):
        got_g(far(base).at[1], 5 + 6 * base)
        send_g(far(base).at[1], 6 + 6 * base, to_xm)

    def near_to_core(base):
        got_g(near(base).at[1], 3 + 6 * base)
        to_partner(near(base), base)

    def far_to_core(base):
        got_g(far(base).at[0], 4 + 6 * base)
        to_partner(far(base), base)

    def other_low():
        got_g(other.at[0], 0)
        send_g(other.at[0], 8, to_xp)
        send_g(other.at[0], 10, to_xm)

    def other_high():
        got_g(other.at[1], 1)
        send_g(other.at[1], 11, to_xm)
        send_g(other.at[1], 9, to_xp)
        to_partner(other, 1)

    def third(base):
        opposite = block(x2, 1 - half if base else half, core)
        got_g(opposite, 6 + 6 * base)
        to_partner(opposite, base)

    def from_core(base):
        got_g(gc.at[0:SEQ], 14 + base)

    def send_a(src, i, to):
        remote(src, src, a_s.at[i], a_r.at[i], to).start()

    def got_a(dst, i):
        remote(dst, dst, a_s.at[i], a_r.at[i], to_core).wait_recv()

    def acts_seq():
        for d in range(3):
            send_a(xa.at[c, s], 0, to_seq[d])

    def begin():
        send_g(mine.at[0], 2, to_xp, 0)
        send_g(mine.at[1], 5, to_xm, 0)
        send_g(mine.at[0], 0, to_half)

    def begin_rest():
        remote(mine, mine, g_s.at[0], g_r.at[0], to_core).wait_send()
        send_g(mine.at[1], 3, to_xp)
        send_g(mine.at[0], 4, to_xm)
        send_g(mine.at[1], 1, to_half)
        to_partner(mine, 0)

    def acts_col():
        got_a(xa.at[c, 0:3], 0)
        send_a(xa.at[c], 1, to_cp)
        send_a(xa.at[c], 1, to_cm)

    def acts_pass():
        got_a(xa.at[0:2], 1)
        send_a(xa.at[cm, 0:2], 2, to_cp)
        send_a(xa.at[cp, 2:4], 2, to_cm)

    lens = [len_ref[q] for q in range(4)]
    first = [jnp.minimum(n, HALF) for n in lens]
    last = [jnp.maximum(n - HALF, 0) for n in lens]

    def runs(start, counts):
        places = []
        for n in counts:
            places.append((start, n))
            start = start + n
        return places, start

    natural_first, n_first = runs(0, first)
    natural_last, _ = runs(n_first, last)
    own, n_own = runs(0, [jnp.where(half == 0, f, l) for f, l in zip(first, last)])
    rest, _ = runs(n_own, [jnp.where(half == 0, l, f) for f, l in zip(first, last)])

    def pick(places, base):
        rows = lax.broadcasted_iota(jnp.int32, (SEQ, HALF), 0) + base
        slot = lax.broadcasted_iota(jnp.int32, (SEQ, HALF), 1)
        tiles = []
        for start_, n in places:
            hit = jnp.logical_and(rows == slot + start_, slot < n)
            tiles.append(jnp.where(hit, 1.0, 0.0).astype(BF16))
        return jnp.concatenate(tiles, axis=1)

    def pack(b):
        parts = []
        if b < 2:
            parts.append((half, pick(own, b * SEQ)))
        if b > 0:
            parts.append((1 - half, pick(rest, b * SEQ)))

        def columns(j, carry):
            cols = pl.ds(pl.multiple_of(j * COLS, COLS), COLS)
            packed = None
            for half_at, chosen in parts:
                rows = xg[:, half_at, :, :, :, cols].reshape(2 * SEQ, COLS)
                one = jnp.dot(chosen, rows, preferred_element_type=F32)
                packed = one if packed is None else packed + one
            gc[b * SEQ : (b + 1) * SEQ, cols] = packed.astype(BF16)
            return carry

        lax.fori_loop(0, chunks, columns, 0)

    def project_inputs():
        got_a(xa.at[0], 2)
        load_ib.wait()
        low = jnp.concatenate([xa[b, q] for q in range(4) for b in (0, 1)], axis=0)
        high = jnp.concatenate([xa[b, q] for q in range(4) for b in (2, 3)], axis=0)
        for b in range(3):
            packed = None
            for use, places, rows in ((b < 2, natural_first, low), (b > 0, natural_last, high)):
                if use:
                    one = jnp.dot(pick(places, b * SEQ), rows, preferred_element_type=F32)
                    packed = one if packed is None else packed + one
            ac[b * SEQ : (b + 1) * SEQ, :] = packed.astype(BF16)
        pa[...] = jnp.dot(ac[...], ib[...], preferred_element_type=F32).reshape(pa.shape)
        send_p(pa.at[1 - core], kr, 0, to_core)

    def send_p(src, dst, i, to):
        remote(src, dst, p_s.at[i], p_r.at[i], to).start()

    def got_p(dst, i):
        remote(dst, dst, p_s.at[i], p_r.at[i], to_core).wait_recv()

    def part(low, high, pf, y1s, y1r, y2s, y2r, zs, zr, gp, c_s, c_r):
        def send(src, dst, i, n, to):
            remote(src, dst, c_s.at[n], c_r.at[i, n], to).start()

        def got(dst, i, n):
            remote(dst, dst, c_s.at[n], c_r.at[i, n], to_core).wait_recv()

        def multiply(i):
            cols = pl.ds(i * COLS if isinstance(i, int) else pl.multiple_of(i * COLS, COLS), COLS)
            pf[i] = jnp.dot(gc[low:high, :], ob[:, cols], preferred_element_type=F32).reshape(pf.shape[1:])
            y1s[i] = pf[i, c2].astype(BF16)
            send(y1s.at[i, 0:2], y1r.at[i, 0], i, 0, to_cp)
            send(y1s.at[i, 2:4], y1r.at[i, 1], i, 0, to_cm)

        def sum_col(i):
            got(y1r.at[i], i, 0)
            y2s[i, 0, 0:2] = (pf[i, cp, 0:2] + y1r[i, 0].astype(F32)).astype(BF16)
            y2s[i, 0, 2:4] = pf[i, cp, 2:4].astype(BF16)
            y2s[i, 1, 0:2] = pf[i, cm, 0:2].astype(BF16)
            y2s[i, 1, 2:4] = (pf[i, cm, 2:4] + y1r[i, 1].astype(F32)).astype(BF16)
            send(y2s.at[i, 0], y2r.at[i, 0], i, 1, to_cp)
            send(y2s.at[i, 1], y2r.at[i, 1], i, 1, to_cm)

        def sum_seq(i):
            got(y2r.at[i], i, 1)
            pf[i, c] = pf[i, c] + y2r[i, 0].astype(F32) + y2r[i, 1].astype(F32)
            zs[i] = pf[i, c].astype(BF16)
            for d in range(3):
                send(zs.at[i, (s + d + 1) % 4], zr.at[i, d], i, 2, to_seq[d])

        def share_seq(i):
            got(zr.at[i], i, 2)
            total = pf[i, c, s]
            for d in range(3):
                total = total + zr[i, d].astype(F32)
            gp[i, c, s] = total.astype(BF16)
            for d in range(3):
                send(gp.at[i, c, s], gp.at[i, c, s], i, 3, to_seq[d])

        def share_col(i):
            got(zr.at[i], i, 3)
            send(gp.at[i, c], gp.at[i, c], i, 4, to_cp)
            send(gp.at[i, c], gp.at[i, c], i, 4, to_cm)

        def pass_col(i):
            got(y2r.at[i], i, 4)
            send(gp.at[i, cm, 0:2], gp.at[i, cm, 0:2], i, 5, to_cp)
            send(gp.at[i, cp, 2:4], gp.at[i, cp, 2:4], i, 5, to_cm)

        def complete(i):
            got(y1r.at[i], i, 5)

        def sent():
            for n, copied in enumerate((y1s, y2s, zr, zr, y2r, y1r)):
                remote(copied, copied, c_s.at[n], c_r.at[0, n], to_core).wait_send()

        return (multiply, sum_col, sum_seq, share_seq, share_col, pass_col), complete, sent

    (multiply0, sum_col0, sum_seq0, share_seq0, share_col0, pass_col0), complete0, sent0 = part(
        0, SEQ, pf0, y1s0, y1r0, y2s0, y2r0, zs0, zr0, gp0, c_s0, c_r0
    )
    (multiply1, sum_col1, sum_seq1, share_seq1, share_col1, pass_col1), complete1, sent1 = part(
        SEQ, LIVE, pf1, y1s1, y1r1, y2s1, y2r1, zs1, zr1, gp1, c_s1, c_r1
    )

    def out_copy(i):
        rows = pl.ds(i * COLS if isinstance(i, int) else pl.multiple_of(i * COLS, COLS), COLS)
        return pltpu.make_async_copy(res.at[i], out_ref.at[rows], out_sem.at[0])

    def square(i):
        complete0(i)
        complete1(i)
        gt[:, 0:SEQ] = gp0[i].reshape(SEQ, COLS).T
        gt[:, SEQ:LIVE] = gp1[i].reshape(LIVE - SEQ, COLS).T
        total = None
        for q in range(4):
            one = jnp.dot(gt[...], am[q], preferred_element_type=F32)
            total = one * one if total is None else total + one * one
        res[i] = total * (1.0 / (4 * SEQ))
        out_copy(i).start()

    def masks():
        got_p(ap.at[1 - core], 7)
        shift = jnp.where(half == 0, 0, LIVE - n_first)
        for b in range(3):
            place = lax.broadcasted_iota(jnp.int32, (SEQ, LIVE), 0) + b * SEQ
            source = lax.broadcasted_iota(jnp.int32, (SEQ, LIVE), 1) + shift
            turn = jnp.logical_or(place == source, place == source - LIVE)
            turn = jnp.where(turn, 1.0, 0.0).astype(BF16)
            turned = jnp.dot(turn, ap[...].reshape(LIVE, ap.shape[-1]), preferred_element_type=F32)
            rows = lax.broadcasted_iota(jnp.int32, turned.shape, 0) + b * SEQ
            for q in range(4):
                inside = jnp.logical_or(
                    jnp.logical_and(rows >= own[q][0], rows < own[q][0] + own[q][1]),
                    jnp.logical_and(rows >= rest[q][0], rows < rest[q][0] + rest[q][1]),
                )
                am[q, b * SEQ : (b + 1) * SEQ, :] = jnp.where(inside, turned, 0.0).astype(BF16)

    def p1():
        got_p(kr, 0)
        pa[core] = pa[core] + kr[...]
        send_p(pa.at[core, x2, 0], x1r.at[0], 1, to_xp)
        send_p(pa.at[core, x2, 1], x1r.at[1], 1, to_xm)

    def p2():
        got_p(x1r, 1)
        pa[core, xp, 0] = pa[core, xp, 0] + x1r[0]
        pa[core, xm, 1] = pa[core, xm, 1] + x1r[1]
        send_p(pa.at[core, xp], x2r.at[0], 2, to_xp)
        send_p(pa.at[core, xm], x2r.at[1], 2, to_xm)

    def p3():
        got_p(x2r, 2)
        pa[core, x] = pa[core, x] + x2r[0] + x2r[1]
        send_p(pa.at[core, x, 1 - half], hr, 3, to_half)

    def p4():
        got_p(hr, 3)
        ap[core, x, half] = (pa[core, x, half] + hr[...]).astype(BF16)
        send_p(ap.at[core, x, half], ap.at[core, x, half], 4, to_half)

    def p5():
        got_p(ap.at[core, x, 1 - half], 4)
        send_p(ap.at[core, x], ap.at[core, x], 5, to_xp)
        send_p(ap.at[core, x], ap.at[core, x], 5, to_xm)

    def p6():
        got_p(ap.at[0, 0:2], 5)
        send_p(ap.at[core, xm, 0], ap.at[core, xm, 0], 6, to_xp)
        send_p(ap.at[core, xp, 1], ap.at[core, xp, 1], 6, to_xm)

    def p7():
        got_p(ap.at[0, 0], 6)
        send_p(ap.at[core], ap.at[core], 7, to_core)

    def each(action, low, high):
        if high - low == 1:
            action(low)
        else:

            def one(i, carry):
                action(i)
                return carry

            lax.fori_loop(low, high, one, 0)

    load_ob.start()
    load_ib.start()
    begin()
    begin_rest()
    relay_low(0)
    relay_high(0)
    near_to_core(0)
    far_to_core(0)
    third(0)
    acts_seq()
    other_low()
    from_core(0)
    pack(0)
    load_ob.wait()
    each(multiply0, 0, 4)
    other_high()
    each(multiply0, 4, 7)
    each(sum_col0, 0, 3)
    relay_low(1)
    each(sum_col0, 3, 7)
    relay_high(1)
    each(sum_seq0, 0, 2)
    near_to_core(1)
    far_to_core(1)
    acts_col()
    each(sum_seq0, 2, 4)
    third(1)
    each(sum_seq0, 4, 6)
    from_core(1)
    pack(1)
    each(sum_seq0, 6, 7)
    acts_pass()
    each(share_seq0, 0, 3)
    pack(2)
    each(multiply1, 0, 3)
    each(share_seq0, 3, 7)
    each(multiply1, 3, 7)
    each(sum_col1, 0, 2)
    project_inputs()
    each(sum_col1, 2, 4)
    each(share_col0, 0, 2)
    each(sum_col1, 4, 7)
    each(sum_seq1, 0, 1)
    p1()
    each(share_col0, 2, 4)
    each(sum_seq1, 1, 2)
    each(pass_col0, 0, 1)
    p2()
    each(share_col0, 4, 7)
    each(share_seq1, 0, 1)
    each(sum_seq1, 2, 3)
    each(pass_col0, 1, 3)
    each(sum_seq1, 3, 4)
    each(share_seq1, 1, 2)
    p3()
    each(sum_seq1, 4, 5)
    each(share_seq1, 2, 3)
    each(share_col1, 0, 1)
    each(pass_col0, 3, 5)
    each(sum_seq1, 5, 6)
    each(share_seq1, 3, 4)
    each(share_col1, 1, 2)
    p4()
    each(sum_seq1, 6, 7)
    each(share_seq1, 4, 5)
    each(share_col1, 2, 3)
    each(pass_col0, 5, 7)
    each(share_seq1, 5, 6)
    each(share_col1, 3, 4)
    each(pass_col1, 0, 1)
    p5()
    each(share_seq1, 6, 7)
    each(share_col1, 4, 5)
    each(pass_col1, 1, 2)
    each(share_col1, 5, 6)
    each(pass_col1, 2, 3)
    p6()
    each(share_col1, 6, 7)
    each(pass_col1, 3, 4)
    p7()
    each(pass_col1, 4, 5)
    masks()
    each(square, 0, 1)
    each(pass_col1, 5, 6)
    each(square, 1, 3)
    each(pass_col1, 6, 7)
    each(square, 3, 7)

    for i, copied in ((1, gc.at[0 : 12 * grads_ref.shape[1]]), (2, gc.at[0 : 16 * grads_ref.shape[1]])):
        remote(copied, copied, g_s.at[i], g_r.at[i], to_core).wait_send()
    for i, copied in enumerate((xa.at[c, 0:3], xa.at[0:2], xa.at[0])):
        remote(copied, copied, a_s.at[i], a_r.at[i], to_core).wait_send()
    for i, copied in enumerate((kr, x1r, x2r, hr, ap.at[0, 0, 0], ap.at[0, 0:2], ap.at[0, 0], ap.at[0])):
        remote(copied, copied, p_s.at[i], p_r.at[i], to_core).wait_send()
    sent0()
    sent1()
    pltpu.make_async_copy(res, res, out_sem.at[0]).wait()


def body(grads, acts, out_basis, in_basis, lengths):
    n_seq, n_col = lax.axis_size("seq"), lax.axis_size("col")
    tokens, width = grads.shape
    a_width = acts.shape[1]
    directions, a_directions = out_basis.shape[1], in_basis.shape[1]
    chunks = directions // COLS
    dma = pltpu.SemaphoreType.DMA

    def part(rows):
        piece = (rows // 16, COLS)
        return [
            pltpu.VMEM((chunks, 4, 4, *piece), F32),
            pltpu.VMEM((chunks, 4, *piece), BF16),
            pltpu.VMEM((chunks, 2, 2, *piece), BF16),
            pltpu.VMEM((chunks, 2, 4, *piece), BF16),
            pltpu.VMEM((chunks, 2, 4, *piece), BF16),
            pltpu.VMEM((chunks, 4, *piece), BF16),
            pltpu.VMEM((chunks, 3, *piece), BF16),
            pltpu.VMEM((chunks, 4, 4, *piece), BF16),
        ]

    hbm = pl.BlockSpec(memory_space=pltpu.HBM)
    return pl.pallas_call(
        functools.partial(kernel, chunks),
        out_shape=jax.ShapeDtypeStruct((directions, a_directions), F32),
        in_specs=[pl.BlockSpec(memory_space=pltpu.SMEM), hbm, hbm, hbm, hbm],
        out_specs=hbm,
        scratch_shapes=[
            pltpu.VMEM((4, 2, 2, 2, tokens // 2, width), BF16),
            pltpu.VMEM((n_col, n_seq, tokens, a_width), BF16),
            pltpu.VMEM(out_basis.shape, BF16),
            pltpu.VMEM(in_basis.shape, BF16),
            pltpu.VMEM((LIVE, width), BF16),
            pltpu.VMEM((LIVE, a_width), BF16),
            *part(SEQ),
            *part(LIVE - SEQ),
            pltpu.VMEM((2, 4, 2, PIECE, a_directions), F32),
            pltpu.VMEM((4, 2, PIECE, a_directions), F32),
            pltpu.VMEM((2, PIECE, a_directions), F32),
            pltpu.VMEM((2, 2, PIECE, a_directions), F32),
            pltpu.VMEM((PIECE, a_directions), F32),
            pltpu.VMEM((2, 4, 2, PIECE, a_directions), BF16),
            pltpu.VMEM((4, LIVE, a_directions), BF16),
            pltpu.VMEM((COLS, LIVE), BF16),
            pltpu.VMEM((chunks, COLS, a_directions), F32),
            dma((4,)),
            dma((1,)),
            dma((3,)),
            dma((16,)),
            dma((3,)),
            dma((3,)),
            dma((8,)),
            dma((8,)),
            dma((6,)),
            dma((chunks, 6)),
            dma((6,)),
            dma((chunks, 6)),
        ],
        compiler_params=pltpu.CompilerParams(
            collective_id=0, has_side_effects=True, vmem_limit_bytes=61730 * 1024
        ),
        name="eigen",
    )(lengths, grads.reshape(2, tokens // 2, width), acts, out_basis, in_basis)


def solution(mesh):
    in_specs = (
        P("row", ("seq", "col")),
        P(("seq", "col"), "row"),
        P(("seq", "col"), "row"),
        P("row", ("seq", "col")),
        P(),
    )
    out_specs = P("row", ("seq", "col"))
    return jax.shard_map(body, mesh=mesh, in_specs=in_specs, out_specs=out_specs, check_vma=False)
```

```python
import functools

import jax
import jax.numpy as jnp
from jax import lax
from jax.experimental import pallas as pl
from jax.experimental.pallas import tpu as pltpu
from jax.sharding import PartitionSpec as P

SEQ = 256
HALF = 128
LIVE = 768
PIECE = 48
COLS = 256
MESH = pl.DeviceIdType.MESH
F32, BF16 = jnp.float32, jnp.bfloat16


def kernel(
    chunks,
    len_ref, grads_ref, acts_ref, ob_ref, ib_ref, out_ref,
    xg, xa, ob, ib, gc, ac,
    pf0, y1s0, y1r0, y2s0, y2r0, zs0, zr0, gp0,
    pf1, y1s1, y1r1, y2s1, y2r1, zs1, zr1, gp1,
    pa, kr, x1r, x2r, hr, ap, am, gt, res,
    loc, out_sem, g_s, g_r, a_s, a_r, p_s, p_r, c_s0, c_r0, c_s1, c_r1,
):
    s, r, c = lax.axis_index("seq"), lax.axis_index("row"), lax.axis_index("col")
    core, half, x = r % 2, (r // 2) % 2, r // 4
    xp, xm, x2 = (x + 1) % 4, (x + 3) % 4, (x + 2) % 4
    cp, cm, c2 = (c + 1) % 4, (c + 3) % 4, (c + 2) % 4

    def row_of(x_at, half_at, core_at):
        return x_at * 4 + half_at * 2 + core_at

    to_core = {"row": row_of(x, half, 1 - core)}
    to_half = {"row": row_of(x, 1 - half, core)}
    to_xp, to_xm = {"row": row_of(xp, half, core)}, {"row": row_of(xm, half, core)}
    to_cp, to_cm = {"col": cp}, {"col": cm}
    even, high_bit = s % 2, s // 2
    to_near, to_far = {"seq": s + 1 - 2 * even}, {"seq": (s + 2) % 4}
    to_seq = [{"seq": (s + d) % 4} for d in (1, 2, 3)]

    def remote(src, dst, send, recv, to):
        return pltpu.make_async_remote_copy(
            src_ref=src, dst_ref=dst, send_sem=send, recv_sem=recv, device_id=to, device_id_type=MESH
        )

    load_g = pltpu.make_async_copy(grads_ref, xg.at[x, half, core], loc.at[0])
    load_a = pltpu.make_async_copy(acts_ref, xa.at[c, s], loc.at[1])
    load_ib = pltpu.make_async_copy(ib_ref, ib, loc.at[2])
    load_ob = pltpu.make_async_copy(ob_ref, ob, loc.at[3])
    load_g.start()
    load_a.start()

    barrier = pltpu.get_barrier_semaphore()
    for to in (to_core, to_half, to_xp, to_xm, to_cp, to_cm, *to_seq):
        pl.semaphore_signal(barrier, inc=1, device_id=to, device_id_type=MESH)
    load_g.wait()
    load_a.wait()
    pl.semaphore_wait(barrier, 9)

    def block(x_at, half_at, core_at):
        return xg.at[x_at, half_at, core_at]

    mine, other = block(x, half, core), block(x, 1 - half, core)
    def send_g(src, recv, to, group=1):
        remote(src, src, g_s.at[group], g_r.at[recv], to).start()

    def to_partner(src, base):
        remote(src, src, g_s.at[2], g_r.at[14 + base], to_core).start()

    def got_g(dst, recv):
        remote(dst, dst, g_s.at[0], g_r.at[recv], to_core).wait_recv()

    def near(base):
        return block(xm, 1 - half if base else half, core)

    def far(base):
        return block(xp, 1 - half if base else half, core)

    def relay_low(base):
        got_g(near(base).at[0], 2 + 6 * base)
        send_g(near(base).at[0], 6 + 6 * base, to_xp)

    def relay_high(base):
        got_g(far(base).at[1], 5 + 6 * base)
        send_g(far(base).at[1], 6 + 6 * base, to_xm)

    def near_to_core(base):
        got_g(near(base).at[1], 3 + 6 * base)
        to_partner(near(base), base)

    def far_to_core(base):
        got_g(far(base).at[0], 4 + 6 * base)
        to_partner(far(base), base)

    def other_low():
        got_g(other.at[0], 0)
        send_g(other.at[0], 8, to_xp)
        send_g(other.at[0], 10, to_xm)

    def other_high():
        got_g(other.at[1], 1)
        send_g(other.at[1], 11, to_xm)
        send_g(other.at[1], 9, to_xp)
        to_partner(other, 1)

    def third(base):
        opposite = block(x2, 1 - half if base else half, core)
        got_g(opposite, 6 + 6 * base)
        to_partner(opposite, base)

    def from_core(base):
        got_g(gc.at[0:SEQ], 14 + base)

    def send_a(src, i, to):
        remote(src, src, a_s.at[i], a_r.at[i], to).start()

    def got_a(dst, i):
        remote(dst, dst, a_s.at[i], a_r.at[i], to_core).wait_recv()

    def acts_seq():
        for d in range(3):
            send_a(xa.at[c, s], 0, to_seq[d])

    def begin():
        send_g(mine.at[0], 2, to_xp, 0)
        send_g(mine.at[1], 5, to_xm, 0)
        send_g(mine.at[0], 0, to_half)

    def begin_rest():
        remote(mine, mine, g_s.at[0], g_r.at[0], to_core).wait_send()
        send_g(mine.at[1], 3, to_xp)
        send_g(mine.at[0], 4, to_xm)
        send_g(mine.at[1], 1, to_half)
        to_partner(mine, 0)

    def acts_col():
        got_a(xa.at[c, 0:3], 0)
        send_a(xa.at[c], 1, to_cp)
        send_a(xa.at[c], 1, to_cm)

    def acts_pass():
        got_a(xa.at[0:2], 1)
        send_a(xa.at[cm, 0:2], 2, to_cp)
        send_a(xa.at[cp, 2:4], 2, to_cm)

    lens = [len_ref[q] for q in range(4)]
    first = [jnp.minimum(n, HALF) for n in lens]
    last = [jnp.maximum(n - HALF, 0) for n in lens]

    def runs(start, counts):
        places = []
        for n in counts:
            places.append((start, n))
            start = start + n
        return places, start

    natural_first, n_first = runs(0, first)
    natural_last, _ = runs(n_first, last)
    own, n_own = runs(0, [jnp.where(half == 0, f, l) for f, l in zip(first, last)])
    rest, _ = runs(n_own, [jnp.where(half == 0, l, f) for f, l in zip(first, last)])

    def pick(places, base):
        rows = lax.broadcasted_iota(jnp.int32, (SEQ, HALF), 0) + base
        slot = lax.broadcasted_iota(jnp.int32, (SEQ, HALF), 1)
        tiles = []
        for start_, n in places:
            hit = jnp.logical_and(rows == slot + start_, slot < n)
            tiles.append(jnp.where(hit, 1.0, 0.0).astype(BF16))
        return jnp.concatenate(tiles, axis=1)

    def pack(b):
        parts = []
        if b < 2:
            parts.append((half, pick(own, b * SEQ)))
        if b > 0:
            parts.append((1 - half, pick(rest, b * SEQ)))

        def columns(j, carry):
            cols = pl.ds(pl.multiple_of(j * COLS, COLS), COLS)
            packed = None
            for half_at, chosen in parts:
                rows = xg[:, half_at, :, :, :, cols].reshape(2 * SEQ, COLS)
                one = jnp.dot(chosen, rows, preferred_element_type=F32)
                packed = one if packed is None else packed + one
            gc[b * SEQ : (b + 1) * SEQ, cols] = packed.astype(BF16)
            return carry

        lax.fori_loop(0, chunks, columns, 0)

    def project_inputs():
        got_a(xa.at[0], 2)
        load_ib.wait()
        low = jnp.concatenate([xa[b, q] for q in range(4) for b in (0, 1)], axis=0)
        high = jnp.concatenate([xa[b, q] for q in range(4) for b in (2, 3)], axis=0)
        for b in range(3):
            packed = None
            for use, places, rows in ((b < 2, natural_first, low), (b > 0, natural_last, high)):
                if use:
                    one = jnp.dot(pick(places, b * SEQ), rows, preferred_element_type=F32)
                    packed = one if packed is None else packed + one
            ac[b * SEQ : (b + 1) * SEQ, :] = packed.astype(BF16)
        wide = pa.shape[-1]
        for h in range(2):
            cols = slice(h * wide, (h + 1) * wide)
            pa[h] = jnp.dot(ac[...], ib[:, cols], preferred_element_type=F32).reshape(pa.shape[1:])
            send_p(pa.at[h, 1 - core], kr.at[h], h, 0, to_core)

    def send_p(src, dst, h, i, to):
        remote(src, dst, p_s.at[i], p_r.at[h, i], to).start()

    def got_p(dst, h, i):
        remote(dst, dst, p_s.at[i], p_r.at[h, i], to_core).wait_recv()

    def part(low, high, pf, y1s, y1r, y2s, y2r, zs, zr, gp, c_s, c_r):
        def send(src, dst, i, n, to):
            remote(src, dst, c_s.at[n], c_r.at[i, n], to).start()

        def got(dst, i, n):
            remote(dst, dst, c_s.at[n], c_r.at[i, n], to_core).wait_recv()

        def multiply(i):
            cols = pl.ds(i * COLS if isinstance(i, int) else pl.multiple_of(i * COLS, COLS), COLS)
            pf[i] = jnp.dot(gc[low:high, :], ob[:, cols], preferred_element_type=F32).reshape(pf.shape[1:])
            y1s[i] = pf[i, c2].astype(BF16)
            send(y1s.at[i, 0:2], y1r.at[i, 0], i, 0, to_cp)
            send(y1s.at[i, 2:4], y1r.at[i, 1], i, 0, to_cm)

        def sum_col(i):
            got(y1r.at[i], i, 0)
            y2s[i, 0, 0:2] = (pf[i, cp, 0:2] + y1r[i, 0].astype(F32)).astype(BF16)
            y2s[i, 0, 2:4] = pf[i, cp, 2:4].astype(BF16)
            y2s[i, 1, 0:2] = pf[i, cm, 0:2].astype(BF16)
            y2s[i, 1, 2:4] = (pf[i, cm, 2:4] + y1r[i, 1].astype(F32)).astype(BF16)
            send(y2s.at[i, 0], y2r.at[i, 0], i, 1, to_cp)
            send(y2s.at[i, 1], y2r.at[i, 1], i, 1, to_cm)

        def sum_seq(i):
            got(y2r.at[i], i, 1)
            pf[i, c] = pf[i, c] + y2r[i, 0].astype(F32) + y2r[i, 1].astype(F32)
            for h in range(2):
                zs[i, h] = pf[i, c, 1 - even + 2 * h].astype(BF16)
            send(zs.at[i, 0:2], zr.at[i, 0:2], i, 2, to_near)

        def pass_seq(i):
            got(zr.at[i, 0:2], i, 2)
            zs[i, 2] = (pf[i, c, even + 2 * (1 - high_bit)] + zr[i, 1 - high_bit].astype(F32)).astype(BF16)
            send(zs.at[i, 2], zr.at[i, 2], i, 6, to_far)
            pf[i, c, s] = pf[i, c, s] + zr[i, high_bit].astype(F32)

        def share_seq(i):
            got(zr.at[i, 2], i, 6)
            gp[i, c, s] = (pf[i, c, s] + zr[i, 2].astype(F32)).astype(BF16)
            for d in range(3):
                send(gp.at[i, c, s], gp.at[i, c, s], i, 3, to_seq[d])

        def share_col(i):
            got(zr.at[i], i, 3)
            send(gp.at[i, c], gp.at[i, c], i, 4, to_cp)
            send(gp.at[i, c], gp.at[i, c], i, 4, to_cm)

        def pass_col(i):
            got(y2r.at[i], i, 4)
            send(gp.at[i, cm, 0:2], gp.at[i, cm, 0:2], i, 5, to_cp)
            send(gp.at[i, cp, 2:4], gp.at[i, cp, 2:4], i, 5, to_cm)

        def complete(i):
            got(y1r.at[i], i, 5)

        def sent():
            for n, copied in enumerate((y1s, y2s, zs.at[:, 0:2], zr, y2r, y1r, zs.at[:, 2])):
                remote(copied, copied, c_s.at[n], c_r.at[0, n], to_core).wait_send()

        return (multiply, sum_col, sum_seq, pass_seq, share_seq, share_col, pass_col), complete, sent

    (multiply0, sum_col0, sum_seq0, pass_seq0, share_seq0, share_col0, pass_col0), complete0, sent0 = part(
        0, SEQ, pf0, y1s0, y1r0, y2s0, y2r0, zs0, zr0, gp0, c_s0, c_r0
    )
    (multiply1, sum_col1, sum_seq1, pass_seq1, share_seq1, share_col1, pass_col1), complete1, sent1 = part(
        SEQ, LIVE, pf1, y1s1, y1r1, y2s1, y2r1, zs1, zr1, gp1, c_s1, c_r1
    )

    def out_copy(i):
        rows = pl.ds(i * COLS if isinstance(i, int) else pl.multiple_of(i * COLS, COLS), COLS)
        return pltpu.make_async_copy(res.at[i], out_ref.at[rows], out_sem.at[0])

    def square(i):
        complete0(i)
        complete1(i)
        gt[:, 0:SEQ] = gp0[i].reshape(SEQ, COLS).T
        gt[:, SEQ:LIVE] = gp1[i].reshape(LIVE - SEQ, COLS).T
        total = None
        for q in range(4):
            one = jnp.dot(gt[...], am[q], preferred_element_type=F32)
            total = one * one if total is None else total + one * one
        res[i] = total * (1.0 / (4 * SEQ))
        out_copy(i).start()

    def masks(h):
        got_p(ap.at[h, 1 - core], h, 7)
        wide = ap.shape[-1]
        shift = jnp.where(half == 0, 0, LIVE - n_first)
        for b in range(3):
            place = lax.broadcasted_iota(jnp.int32, (SEQ, LIVE), 0) + b * SEQ
            source = lax.broadcasted_iota(jnp.int32, (SEQ, LIVE), 1) + shift
            turn = jnp.logical_or(place == source, place == source - LIVE)
            turn = jnp.where(turn, 1.0, 0.0).astype(BF16)
            turned = jnp.dot(turn, ap[h].reshape(LIVE, wide), preferred_element_type=F32)
            rows = lax.broadcasted_iota(jnp.int32, turned.shape, 0) + b * SEQ
            for q in range(4):
                inside = jnp.logical_or(
                    jnp.logical_and(rows >= own[q][0], rows < own[q][0] + own[q][1]),
                    jnp.logical_and(rows >= rest[q][0], rows < rest[q][0] + rest[q][1]),
                )
                am[q, b * SEQ : (b + 1) * SEQ, h * wide : (h + 1) * wide] = jnp.where(inside, turned, 0.0).astype(BF16)

    def p1(h):
        got_p(kr.at[h], h, 0)
        pa[h, core] = pa[h, core] + kr[h]
        send_p(pa.at[h, core, x2, 0], x1r.at[h, 0], h, 1, to_xp)
        send_p(pa.at[h, core, x2, 1], x1r.at[h, 1], h, 1, to_xm)

    def p2(h):
        got_p(x1r.at[h], h, 1)
        pa[h, core, xp, 0] = pa[h, core, xp, 0] + x1r[h, 0]
        pa[h, core, xm, 1] = pa[h, core, xm, 1] + x1r[h, 1]
        send_p(pa.at[h, core, xp], x2r.at[h, 0], h, 2, to_xp)
        send_p(pa.at[h, core, xm], x2r.at[h, 1], h, 2, to_xm)

    def p3(h):
        got_p(x2r.at[h], h, 2)
        pa[h, core, x] = pa[h, core, x] + x2r[h, 0] + x2r[h, 1]
        send_p(pa.at[h, core, x, 1 - half], hr.at[h], h, 3, to_half)

    def p4(h):
        got_p(hr.at[h], h, 3)
        ap[h, core, x, half] = (pa[h, core, x, half] + hr[h]).astype(BF16)
        send_p(ap.at[h, core, x, half], ap.at[h, core, x, half], h, 4, to_half)

    def p5(h):
        got_p(ap.at[h, core, x, 1 - half], h, 4)
        send_p(ap.at[h, core, x], ap.at[h, core, x], h, 5, to_xp)
        send_p(ap.at[h, core, x], ap.at[h, core, x], h, 5, to_xm)

    def p6(h):
        got_p(ap.at[h, 0, 0:2], h, 5)
        send_p(ap.at[h, core, xm, 0], ap.at[h, core, xm, 0], h, 6, to_xp)
        send_p(ap.at[h, core, xp, 1], ap.at[h, core, xp, 1], h, 6, to_xm)

    def p7(h):
        got_p(ap.at[h, 0, 0], h, 6)
        send_p(ap.at[h, core], ap.at[h, core], h, 7, to_core)

    def each(action, low, high):
        if high - low == 1:
            action(low)
        else:

            def one(i, carry):
                action(i)
                return carry

            lax.fori_loop(low, high, one, 0)

    load_ob.start()
    load_ib.start()
    begin()
    begin_rest()
    relay_low(0)
    relay_high(0)
    near_to_core(0)
    far_to_core(0)
    third(0)
    acts_seq()
    other_low()
    from_core(0)
    pack(0)
    load_ob.wait()
    each(multiply0, 0, 4)
    other_high()
    each(multiply0, 4, 7)
    each(sum_col0, 0, 3)
    relay_low(1)
    each(sum_col0, 3, 7)
    relay_high(1)
    each(sum_seq0, 0, 2)
    acts_col()
    near_to_core(1)
    far_to_core(1)
    each(sum_seq0, 2, 4)
    third(1)
    each(sum_seq0, 4, 6)
    from_core(1)
    pack(1)
    each(sum_seq0, 6, 7)
    each(pass_seq0, 0, 5)
    pack(2)
    acts_pass()
    each(pass_seq0, 5, 7)
    each(share_seq0, 0, 3)
    each(multiply1, 0, 5)
    each(share_seq0, 3, 7)
    each(multiply1, 5, 7)
    each(sum_col1, 0, 2)
    project_inputs()
    each(sum_col1, 2, 7)
    p1(0)
    p1(1)
    each(sum_seq1, 0, 1)
    each(share_col0, 0, 2)
    each(sum_seq1, 1, 2)
    p2(0)
    each(pass_seq1, 0, 1)
    p2(1)
    each(sum_seq1, 2, 3)
    each(pass_seq1, 1, 2)
    p3(0)
    each(share_col0, 2, 4)
    each(share_seq1, 0, 1)
    p3(1)
    each(sum_seq1, 3, 4)
    each(pass_seq1, 2, 3)
    each(share_seq1, 1, 2)
    each(share_col0, 4, 7)
    each(sum_seq1, 4, 5)
    each(sum_seq1, 5, 6)
    each(pass_col0, 0, 2)
    each(sum_seq1, 6, 7)
    p4(0)
    each(pass_seq1, 3, 4)
    each(share_seq1, 2, 3)
    p4(1)
    each(pass_seq1, 4, 5)
    each(pass_col0, 2, 4)
    each(pass_seq1, 5, 6)
    each(share_col1, 0, 1)
    each(share_seq1, 3, 4)
    each(pass_seq1, 6, 7)
    p5(0)
    each(share_col1, 1, 2)
    each(share_seq1, 4, 5)
    p5(1)
    each(pass_col0, 4, 7)
    each(share_seq1, 5, 6)
    each(share_col1, 2, 3)
    each(share_seq1, 6, 7)
    p6(0)
    each(share_col1, 3, 4)
    p6(1)
    each(pass_col1, 0, 1)
    each(share_col1, 4, 5)
    p7(0)
    each(pass_col1, 1, 2)
    p7(1)
    each(share_col1, 5, 6)
    masks(0)
    each(pass_col1, 2, 3)
    each(share_col1, 6, 7)
    masks(1)
    each(pass_col1, 3, 4)
    each(square, 0, 1)
    each(pass_col1, 4, 5)
    each(square, 1, 2)
    each(pass_col1, 5, 6)
    each(square, 2, 3)
    each(pass_col1, 6, 7)
    each(square, 3, 7)

    for i, copied in ((1, gc.at[0 : 12 * grads_ref.shape[1]]), (2, gc.at[0 : 16 * grads_ref.shape[1]])):
        remote(copied, copied, g_s.at[i], g_r.at[i], to_core).wait_send()
    for i, copied in enumerate((xa.at[c, 0:3], xa.at[0:2], xa.at[0])):
        remote(copied, copied, a_s.at[i], a_r.at[i], to_core).wait_send()
    for i, copied in enumerate((kr, x1r, x2r, hr, ap.at[:, 0, 0, 0], ap.at[:, 0, 0:2], ap.at[:, 0, 0], ap.at[:, 0])):
        remote(copied, copied, p_s.at[i], p_r.at[0, i], to_core).wait_send()
    sent0()
    sent1()
    pltpu.make_async_copy(res, res, out_sem.at[0]).wait()


def body(grads, acts, out_basis, in_basis, lengths):
    n_seq, n_col = lax.axis_size("seq"), lax.axis_size("col")
    tokens, width = grads.shape
    a_width = acts.shape[1]
    directions, a_directions = out_basis.shape[1], in_basis.shape[1]
    chunks = directions // COLS
    dma = pltpu.SemaphoreType.DMA

    def part(rows):
        piece = (rows // 16, COLS)
        return [
            pltpu.VMEM((chunks, 4, 4, *piece), F32),
            pltpu.VMEM((chunks, 4, *piece), BF16),
            pltpu.VMEM((chunks, 2, 2, *piece), BF16),
            pltpu.VMEM((chunks, 2, 4, *piece), BF16),
            pltpu.VMEM((chunks, 2, 4, *piece), BF16),
            pltpu.VMEM((chunks, 3, *piece), BF16),
            pltpu.VMEM((chunks, 3, *piece), BF16),
            pltpu.VMEM((chunks, 4, 4, *piece), BF16),
        ]

    a_piece = (PIECE, a_directions // 2)
    hbm = pl.BlockSpec(memory_space=pltpu.HBM)
    return pl.pallas_call(
        functools.partial(kernel, chunks),
        out_shape=jax.ShapeDtypeStruct((directions, a_directions), F32),
        in_specs=[pl.BlockSpec(memory_space=pltpu.SMEM), hbm, hbm, hbm, hbm],
        out_specs=hbm,
        scratch_shapes=[
            pltpu.VMEM((4, 2, 2, 2, tokens // 2, width), BF16),
            pltpu.VMEM((n_col, n_seq, tokens, a_width), BF16),
            pltpu.VMEM(out_basis.shape, BF16),
            pltpu.VMEM(in_basis.shape, BF16),
            pltpu.VMEM((LIVE, width), BF16),
            pltpu.VMEM((LIVE, a_width), BF16),
            *part(SEQ),
            *part(LIVE - SEQ),
            pltpu.VMEM((2, 2, 4, 2, *a_piece), F32),
            pltpu.VMEM((2, 4, 2, *a_piece), F32),
            pltpu.VMEM((2, 2, *a_piece), F32),
            pltpu.VMEM((2, 2, 2, *a_piece), F32),
            pltpu.VMEM((2, *a_piece), F32),
            pltpu.VMEM((2, 2, 4, 2, *a_piece), BF16),
            pltpu.VMEM((4, LIVE, a_directions), BF16),
            pltpu.VMEM((COLS, LIVE), BF16),
            pltpu.VMEM((chunks, COLS, a_directions), F32),
            dma((4,)),
            dma((1,)),
            dma((3,)),
            dma((16,)),
            dma((3,)),
            dma((3,)),
            dma((8,)),
            dma((2, 8)),
            dma((7,)),
            dma((chunks, 7)),
            dma((7,)),
            dma((chunks, 7)),
        ],
        compiler_params=pltpu.CompilerParams(
            collective_id=0, has_side_effects=True, vmem_limit_bytes=61730 * 1024
        ),
        name="eigen",
    )(lengths, grads.reshape(2, tokens // 2, width), acts, out_basis, in_basis)


def solution(mesh):
    in_specs = (
        P("row", ("seq", "col")),
        P(("seq", "col"), "row"),
        P(("seq", "col"), "row"),
        P("row", ("seq", "col")),
        P(),
    )
    out_specs = P("row", ("seq", "col"))
    return jax.shard_map(body, mesh=mesh, in_specs=in_specs, out_specs=out_specs, check_vma=False)
```

```python
import functools

import jax
import jax.numpy as jnp
from jax import lax
from jax.experimental import pallas as pl
from jax.experimental.pallas import tpu as pltpu
from jax.sharding import PartitionSpec as P

SEQ = 256
HALF = 128
LIVE = 768
PIECE = 48
COLS = 256
MESH = pl.DeviceIdType.MESH
F32, BF16 = jnp.float32, jnp.bfloat16


def kernel(
    chunks,
    len_ref, grads_ref, acts_ref, ob_ref, ib_ref, out_ref,
    xg, xa, ob, ib, gc, ac,
    pf0, y1s0, y1r0, y2s0, y2r0, zs0, zr0, gp0,
    pf1, y1s1, y1r1, y2s1, y2r1, zs1, zr1, gp1,
    pa, kr, x1r, x2r, hr, ap, am, gt, res,
    loc, out_sem, g_s, g_r, a_s, a_r, p_s, p_r, c_s0, c_r0, c_s1, c_r1,
):
    s, r, c = lax.axis_index("seq"), lax.axis_index("row"), lax.axis_index("col")
    core, half, x = r % 2, (r // 2) % 2, r // 4
    xp, xm, x2 = (x + 1) % 4, (x + 3) % 4, (x + 2) % 4
    cp, cm, c2 = (c + 1) % 4, (c + 3) % 4, (c + 2) % 4

    def row_of(x_at, half_at, core_at):
        return x_at * 4 + half_at * 2 + core_at

    to_core = {"row": row_of(x, half, 1 - core)}
    to_half = {"row": row_of(x, 1 - half, core)}
    to_xp, to_xm = {"row": row_of(xp, half, core)}, {"row": row_of(xm, half, core)}
    to_cp, to_cm = {"col": cp}, {"col": cm}
    even, high_bit = s % 2, s // 2
    to_near, to_far = {"seq": s + 1 - 2 * even}, {"seq": (s + 2) % 4}
    to_seq = [{"seq": (s + d) % 4} for d in (1, 2, 3)]

    def remote(src, dst, send, recv, to):
        return pltpu.make_async_remote_copy(
            src_ref=src, dst_ref=dst, send_sem=send, recv_sem=recv, device_id=to, device_id_type=MESH
        )

    load_g = pltpu.make_async_copy(grads_ref, xg.at[x, half, core], loc.at[0])
    load_a = pltpu.make_async_copy(acts_ref, xa.at[c, s], loc.at[1])
    load_ib = pltpu.make_async_copy(ib_ref, ib, loc.at[2])
    load_ob = pltpu.make_async_copy(ob_ref, ob, loc.at[3])
    load_g.start()
    load_a.start()

    barrier = pltpu.get_barrier_semaphore()
    for to in (to_core, to_half, to_xp, to_xm, to_cp, to_cm, *to_seq):
        pl.semaphore_signal(barrier, inc=1, device_id=to, device_id_type=MESH)
    load_g.wait()
    load_a.wait()
    pl.semaphore_wait(barrier, 9)

    def block(x_at, half_at, core_at):
        return xg.at[x_at, half_at, core_at]

    mine, other = block(x, half, core), block(x, 1 - half, core)
    def send_g(src, recv, to, group=1):
        remote(src, src, g_s.at[group], g_r.at[recv], to).start()

    def to_partner(src, base):
        remote(src, src, g_s.at[2], g_r.at[14 + base], to_core).start()

    def got_g(dst, recv):
        remote(dst, dst, g_s.at[0], g_r.at[recv], to_core).wait_recv()

    def near(base):
        return block(xm, 1 - half if base else half, core)

    def far(base):
        return block(xp, 1 - half if base else half, core)

    def relay_low(base):
        got_g(near(base).at[0], 2 + 6 * base)
        send_g(near(base).at[0], 6 + 6 * base, to_xp)

    def relay_high(base):
        got_g(far(base).at[1], 5 + 6 * base)
        send_g(far(base).at[1], 6 + 6 * base, to_xm)

    def near_to_core(base):
        got_g(near(base).at[1], 3 + 6 * base)
        to_partner(near(base), base)

    def far_to_core(base):
        got_g(far(base).at[0], 4 + 6 * base)
        to_partner(far(base), base)

    def other_low():
        got_g(other.at[0], 0)
        send_g(other.at[0], 8, to_xp)
        send_g(other.at[0], 10, to_xm)

    def other_high():
        got_g(other.at[1], 1)
        send_g(other.at[1], 11, to_xm)
        send_g(other.at[1], 9, to_xp)
        to_partner(other, 1)

    def third(base):
        opposite = block(x2, 1 - half if base else half, core)
        got_g(opposite, 6 + 6 * base)
        to_partner(opposite, base)

    def from_core(base):
        got_g(gc.at[0:SEQ], 14 + base)

    def send_a(src, i, to):
        remote(src, src, a_s.at[i], a_r.at[i], to).start()

    def got_a(dst, i):
        remote(dst, dst, a_s.at[i], a_r.at[i], to_core).wait_recv()

    def acts_seq():
        for d in range(3):
            send_a(xa.at[c, s], 0, to_seq[d])

    def begin():
        send_g(mine.at[0], 2, to_xp, 0)
        send_g(mine.at[1], 5, to_xm, 0)
        send_g(mine.at[0], 0, to_half)

    def begin_rest():
        remote(mine, mine, g_s.at[0], g_r.at[0], to_core).wait_send()
        send_g(mine.at[1], 3, to_xp)
        send_g(mine.at[0], 4, to_xm)
        send_g(mine.at[1], 1, to_half)
        to_partner(mine, 0)

    def acts_col():
        got_a(xa.at[c, 0:3], 0)
        send_a(xa.at[c], 1, to_cp)
        send_a(xa.at[c], 1, to_cm)

    def acts_pass():
        got_a(xa.at[0:2], 1)
        send_a(xa.at[cm, 0:2], 2, to_cp)
        send_a(xa.at[cp, 2:4], 2, to_cm)

    lens = [len_ref[q] for q in range(4)]
    first = [jnp.minimum(n, HALF) for n in lens]
    last = [jnp.maximum(n - HALF, 0) for n in lens]

    def runs(start, counts):
        places = []
        for n in counts:
            places.append((start, n))
            start = start + n
        return places, start

    natural_first, n_first = runs(0, first)
    natural_last, _ = runs(n_first, last)
    own, n_own = runs(0, [jnp.where(half == 0, f, l) for f, l in zip(first, last)])
    rest, _ = runs(n_own, [jnp.where(half == 0, l, f) for f, l in zip(first, last)])

    def pick(places, base):
        rows = lax.broadcasted_iota(jnp.int32, (SEQ, HALF), 0) + base
        slot = lax.broadcasted_iota(jnp.int32, (SEQ, HALF), 1)
        tiles = []
        for start_, n in places:
            hit = jnp.logical_and(rows == slot + start_, slot < n)
            tiles.append(jnp.where(hit, 1.0, 0.0).astype(BF16))
        return jnp.concatenate(tiles, axis=1)

    def pack(b):
        parts = []
        if b < 2:
            parts.append((half, pick(own, b * SEQ)))
        if b > 0:
            parts.append((1 - half, pick(rest, b * SEQ)))

        def columns(j, carry):
            cols = pl.ds(pl.multiple_of(j * COLS, COLS), COLS)
            packed = None
            for half_at, chosen in parts:
                rows = xg[:, half_at, :, :, :, cols].reshape(2 * SEQ, COLS)
                one = jnp.dot(chosen, rows, preferred_element_type=F32)
                packed = one if packed is None else packed + one
            gc[b * SEQ : (b + 1) * SEQ, cols] = packed.astype(BF16)
            return carry

        lax.fori_loop(0, chunks, columns, 0)

    def project_inputs():
        got_a(xa.at[0], 2)
        load_ib.wait()
        low = jnp.concatenate([xa[b, q] for q in range(4) for b in (0, 1)], axis=0)
        high = jnp.concatenate([xa[b, q] for q in range(4) for b in (2, 3)], axis=0)
        for b in range(3):
            packed = None
            for use, places, rows in ((b < 2, natural_first, low), (b > 0, natural_last, high)):
                if use:
                    one = jnp.dot(pick(places, b * SEQ), rows, preferred_element_type=F32)
                    packed = one if packed is None else packed + one
            ac[b * SEQ : (b + 1) * SEQ, :] = packed.astype(BF16)
        wide = pa.shape[-1]
        for h in range(2):
            cols = slice(h * wide, (h + 1) * wide)
            pa[h] = jnp.dot(ac[...], ib[:, cols], preferred_element_type=F32).reshape(pa.shape[1:])
            send_p(pa.at[h, 1 - core], kr.at[h], h, 0, to_core)

    def send_p(src, dst, h, i, to):
        remote(src, dst, p_s.at[i], p_r.at[h, i], to).start()

    def got_p(dst, h, i):
        remote(dst, dst, p_s.at[i], p_r.at[h, i], to_core).wait_recv()

    def part(low, high, pf, y1s, y1r, y2s, y2r, zs, zr, gp, c_s, c_r):
        def send(src, dst, i, n, to):
            remote(src, dst, c_s.at[n], c_r.at[i, n], to).start()

        def got(dst, i, n):
            remote(dst, dst, c_s.at[n], c_r.at[i, n], to_core).wait_recv()

        def multiply(i):
            cols = pl.ds(i * COLS if isinstance(i, int) else pl.multiple_of(i * COLS, COLS), COLS)
            pf[i] = jnp.dot(gc[low:high, :], ob[:, cols], preferred_element_type=F32).reshape(pf.shape[1:])
            y1s[i] = pf[i, c2].astype(BF16)
            send(y1s.at[i, 0:2], y1r.at[i, 0], i, 0, to_cp)
            send(y1s.at[i, 2:4], y1r.at[i, 1], i, 0, to_cm)

        def sum_col(i):
            got(y1r.at[i], i, 0)
            y2s[i, 0, 0:2] = (pf[i, cp, 0:2] + y1r[i, 0].astype(F32)).astype(BF16)
            y2s[i, 0, 2:4] = pf[i, cp, 2:4].astype(BF16)
            y2s[i, 1, 0:2] = pf[i, cm, 0:2].astype(BF16)
            y2s[i, 1, 2:4] = (pf[i, cm, 2:4] + y1r[i, 1].astype(F32)).astype(BF16)
            send(y2s.at[i, 0], y2r.at[i, 0], i, 1, to_cp)
            send(y2s.at[i, 1], y2r.at[i, 1], i, 1, to_cm)

        def sum_seq(i):
            got(y2r.at[i], i, 1)
            pf[i, c] = pf[i, c] + y2r[i, 0].astype(F32) + y2r[i, 1].astype(F32)
            for h in range(2):
                zs[i, h] = pf[i, c, 1 - even + 2 * h].astype(BF16)
            send(zs.at[i, 0:2], zr.at[i, 0:2], i, 2, to_near)

        def pass_seq(i):
            got(zr.at[i, 0:2], i, 2)
            zs[i, 2] = (pf[i, c, even + 2 * (1 - high_bit)] + zr[i, 1 - high_bit].astype(F32)).astype(BF16)
            send(zs.at[i, 2], zr.at[i, 2], i, 6, to_far)
            pf[i, c, s] = pf[i, c, s] + zr[i, high_bit].astype(F32)

        def share_seq(i):
            got(zr.at[i, 2], i, 6)
            gp[i, c, s] = (pf[i, c, s] + zr[i, 2].astype(F32)).astype(BF16)
            for d in range(3):
                send(gp.at[i, c, s], gp.at[i, c, s], i, 3, to_seq[d])

        def share_col(i):
            got(zr.at[i], i, 3)
            send(gp.at[i, c], gp.at[i, c], i, 4, to_cp)
            send(gp.at[i, c], gp.at[i, c], i, 4, to_cm)

        def pass_col(i):
            got(y2r.at[i], i, 4)
            send(gp.at[i, cm, 0:2], gp.at[i, cm, 0:2], i, 5, to_cp)
            send(gp.at[i, cp, 2:4], gp.at[i, cp, 2:4], i, 5, to_cm)

        def complete(i):
            got(y1r.at[i], i, 5)

        def sent():
            for n, copied in enumerate((y1s, y2s, zs.at[:, 0:2], zr, y2r, y1r, zs.at[:, 2])):
                remote(copied, copied, c_s.at[n], c_r.at[0, n], to_core).wait_send()

        return (multiply, sum_col, sum_seq, pass_seq, share_seq, share_col, pass_col), complete, sent

    (multiply0, sum_col0, sum_seq0, pass_seq0, share_seq0, share_col0, pass_col0), complete0, sent0 = part(
        0, SEQ, pf0, y1s0, y1r0, y2s0, y2r0, zs0, zr0, gp0, c_s0, c_r0
    )
    (multiply1, sum_col1, sum_seq1, pass_seq1, share_seq1, share_col1, pass_col1), complete1, sent1 = part(
        SEQ, LIVE, pf1, y1s1, y1r1, y2s1, y2r1, zs1, zr1, gp1, c_s1, c_r1
    )

    def out_copy(i):
        rows = pl.ds(i * COLS if isinstance(i, int) else pl.multiple_of(i * COLS, COLS), COLS)
        return pltpu.make_async_copy(res.at[i], out_ref.at[rows], out_sem.at[0])

    def square(i):
        complete0(i)
        complete1(i)
        gt[:, 0:SEQ] = gp0[i].reshape(SEQ, COLS).T
        gt[:, SEQ:LIVE] = gp1[i].reshape(LIVE - SEQ, COLS).T
        total = None
        for q in range(4):
            one = jnp.dot(gt[...], am[q], preferred_element_type=F32)
            total = one * one if total is None else total + one * one
        res[i] = total * (1.0 / (4 * SEQ))
        out_copy(i).start()

    def masks(h):
        got_p(ap.at[h, 1 - core], h, 7)
        wide = ap.shape[-1]
        shift = jnp.where(half == 0, 0, LIVE - n_first)
        for b in range(3):
            place = lax.broadcasted_iota(jnp.int32, (SEQ, LIVE), 0) + b * SEQ
            source = lax.broadcasted_iota(jnp.int32, (SEQ, LIVE), 1) + shift
            turn = jnp.logical_or(place == source, place == source - LIVE)
            turn = jnp.where(turn, 1.0, 0.0).astype(BF16)
            turned = jnp.dot(turn, ap[h].reshape(LIVE, wide), preferred_element_type=F32)
            rows = lax.broadcasted_iota(jnp.int32, turned.shape, 0) + b * SEQ
            for q in range(4):
                inside = jnp.logical_or(
                    jnp.logical_and(rows >= own[q][0], rows < own[q][0] + own[q][1]),
                    jnp.logical_and(rows >= rest[q][0], rows < rest[q][0] + rest[q][1]),
                )
                am[q, b * SEQ : (b + 1) * SEQ, h * wide : (h + 1) * wide] = jnp.where(inside, turned, 0.0).astype(BF16)

    def p1(h):
        got_p(kr.at[h], h, 0)
        pa[h, core] = pa[h, core] + kr[h]
        send_p(pa.at[h, core, x2, 0], x1r.at[h, 0], h, 1, to_xp)
        send_p(pa.at[h, core, x2, 1], x1r.at[h, 1], h, 1, to_xm)

    def p2(h):
        got_p(x1r.at[h], h, 1)
        pa[h, core, xp, 0] = pa[h, core, xp, 0] + x1r[h, 0]
        pa[h, core, xm, 1] = pa[h, core, xm, 1] + x1r[h, 1]
        send_p(pa.at[h, core, xp], x2r.at[h, 0], h, 2, to_xp)
        send_p(pa.at[h, core, xm], x2r.at[h, 1], h, 2, to_xm)

    def p3(h):
        got_p(x2r.at[h], h, 2)
        pa[h, core, x] = pa[h, core, x] + x2r[h, 0] + x2r[h, 1]
        send_p(pa.at[h, core, x, 1 - half], hr.at[h], h, 3, to_half)

    def p4(h):
        got_p(hr.at[h], h, 3)
        ap[h, core, x, half] = (pa[h, core, x, half] + hr[h]).astype(BF16)
        send_p(ap.at[h, core, x, half], ap.at[h, core, x, half], h, 4, to_half)

    def p5(h):
        got_p(ap.at[h, core, x, 1 - half], h, 4)
        send_p(ap.at[h, core, x], ap.at[h, core, x], h, 5, to_xp)
        send_p(ap.at[h, core, x], ap.at[h, core, x], h, 5, to_xm)

    def p6(h):
        got_p(ap.at[h, 0, 0:2], h, 5)
        send_p(ap.at[h, core, xm, 0], ap.at[h, core, xm, 0], h, 6, to_xp)
        send_p(ap.at[h, core, xp, 1], ap.at[h, core, xp, 1], h, 6, to_xm)

    def p7(h):
        got_p(ap.at[h, 0, 0], h, 6)
        send_p(ap.at[h, core], ap.at[h, core], h, 7, to_core)

    def each(action, low, high):
        if high - low == 1:
            action(low)
        else:

            def one(i, carry):
                action(i)
                return carry

            lax.fori_loop(low, high, one, 0)

    load_ob.start()
    load_ib.start()
    begin()
    begin_rest()
    relay_low(0)
    relay_high(0)
    near_to_core(0)
    far_to_core(0)
    third(0)
    acts_seq()
    other_low()
    from_core(0)
    pack(0)
    load_ob.wait()
    each(multiply0, 0, 4)
    other_high()
    each(multiply0, 4, 7)
    each(sum_col0, 0, 3)
    relay_low(1)
    each(sum_col0, 3, 7)
    relay_high(1)
    each(sum_seq0, 0, 2)
    acts_col()
    near_to_core(1)
    far_to_core(1)
    each(sum_seq0, 2, 4)
    third(1)
    each(sum_seq0, 4, 6)
    from_core(1)
    pack(1)
    each(sum_seq0, 6, 7)
    each(pass_seq0, 0, 5)
    pack(2)
    acts_pass()
    each(pass_seq0, 5, 7)
    each(share_seq0, 0, 3)
    each(multiply1, 0, 5)
    each(share_seq0, 3, 7)
    each(multiply1, 5, 7)
    each(sum_col1, 0, 2)
    project_inputs()
    each(sum_col1, 2, 7)
    p1(0)
    p1(1)
    each(sum_seq1, 0, 1)
    each(share_col0, 0, 2)
    each(sum_seq1, 1, 2)
    p2(0)
    each(pass_seq1, 0, 1)
    p2(1)
    each(sum_seq1, 2, 3)
    each(pass_seq1, 1, 2)
    p3(0)
    each(share_col0, 2, 4)
    each(share_seq1, 0, 1)
    p3(1)
    each(sum_seq1, 3, 4)
    each(pass_seq1, 2, 3)
    each(share_seq1, 1, 2)
    each(share_col0, 4, 7)
    each(sum_seq1, 4, 5)
    each(sum_seq1, 5, 6)
    each(pass_col0, 0, 2)
    each(sum_seq1, 6, 7)
    p4(0)
    p4(1)
    each(pass_seq1, 3, 4)
    each(share_seq1, 2, 3)
    each(pass_seq1, 4, 5)
    each(pass_col0, 2, 4)
    each(pass_seq1, 5, 6)
    each(share_col1, 0, 1)
    each(share_seq1, 3, 4)
    each(pass_seq1, 6, 7)
    p5(0)
    each(share_col1, 1, 2)
    each(share_seq1, 4, 5)
    p5(1)
    each(pass_col0, 4, 7)
    each(share_seq1, 5, 6)
    each(share_col1, 2, 3)
    each(share_seq1, 6, 7)
    p6(0)
    each(share_col1, 3, 4)
    each(share_col1, 4, 5)
    p6(1)
    each(pass_col1, 0, 1)
    each(share_col1, 5, 6)
    p7(0)
    each(pass_col1, 1, 2)
    each(share_col1, 6, 7)
    p7(1)
    masks(0)
    each(pass_col1, 2, 3)
    masks(1)
    each(pass_col1, 3, 4)
    each(square, 0, 1)
    each(pass_col1, 4, 5)
    each(square, 1, 2)
    each(pass_col1, 5, 6)
    each(square, 2, 3)
    each(pass_col1, 6, 7)
    each(square, 3, 7)

    for i, copied in ((1, gc.at[0 : 12 * grads_ref.shape[1]]), (2, gc.at[0 : 16 * grads_ref.shape[1]])):
        remote(copied, copied, g_s.at[i], g_r.at[i], to_core).wait_send()
    for i, copied in enumerate((xa.at[c, 0:3], xa.at[0:2], xa.at[0])):
        remote(copied, copied, a_s.at[i], a_r.at[i], to_core).wait_send()
    for i, copied in enumerate((kr, x1r, x2r, hr, ap.at[:, 0, 0, 0], ap.at[:, 0, 0:2], ap.at[:, 0, 0], ap.at[:, 0])):
        remote(copied, copied, p_s.at[i], p_r.at[0, i], to_core).wait_send()
    sent0()
    sent1()
    pltpu.make_async_copy(res, res, out_sem.at[0]).wait()


def body(grads, acts, out_basis, in_basis, lengths):
    n_seq, n_col = lax.axis_size("seq"), lax.axis_size("col")
    tokens, width = grads.shape
    a_width = acts.shape[1]
    directions, a_directions = out_basis.shape[1], in_basis.shape[1]
    chunks = directions // COLS
    dma = pltpu.SemaphoreType.DMA

    def part(rows):
        piece = (rows // 16, COLS)
        return [
            pltpu.VMEM((chunks, 4, 4, *piece), F32),
            pltpu.VMEM((chunks, 4, *piece), BF16),
            pltpu.VMEM((chunks, 2, 2, *piece), BF16),
            pltpu.VMEM((chunks, 2, 4, *piece), BF16),
            pltpu.VMEM((chunks, 2, 4, *piece), BF16),
            pltpu.VMEM((chunks, 3, *piece), BF16),
            pltpu.VMEM((chunks, 3, *piece), BF16),
            pltpu.VMEM((chunks, 4, 4, *piece), BF16),
        ]

    a_piece = (PIECE, a_directions // 2)
    hbm = pl.BlockSpec(memory_space=pltpu.HBM)
    return pl.pallas_call(
        functools.partial(kernel, chunks),
        out_shape=jax.ShapeDtypeStruct((directions, a_directions), F32),
        in_specs=[pl.BlockSpec(memory_space=pltpu.SMEM), hbm, hbm, hbm, hbm],
        out_specs=hbm,
        scratch_shapes=[
            pltpu.VMEM((4, 2, 2, 2, tokens // 2, width), BF16),
            pltpu.VMEM((n_col, n_seq, tokens, a_width), BF16),
            pltpu.VMEM(out_basis.shape, BF16),
            pltpu.VMEM(in_basis.shape, BF16),
            pltpu.VMEM((LIVE, width), BF16),
            pltpu.VMEM((LIVE, a_width), BF16),
            *part(SEQ),
            *part(LIVE - SEQ),
            pltpu.VMEM((2, 2, 4, 2, *a_piece), F32),
            pltpu.VMEM((2, 4, 2, *a_piece), F32),
            pltpu.VMEM((2, 2, *a_piece), F32),
            pltpu.VMEM((2, 2, 2, *a_piece), F32),
            pltpu.VMEM((2, *a_piece), F32),
            pltpu.VMEM((2, 2, 4, 2, *a_piece), BF16),
            pltpu.VMEM((4, LIVE, a_directions), BF16),
            pltpu.VMEM((COLS, LIVE), BF16),
            pltpu.VMEM((chunks, COLS, a_directions), F32),
            dma((4,)),
            dma((1,)),
            dma((3,)),
            dma((16,)),
            dma((3,)),
            dma((3,)),
            dma((8,)),
            dma((2, 8)),
            dma((7,)),
            dma((chunks, 7)),
            dma((7,)),
            dma((chunks, 7)),
        ],
        compiler_params=pltpu.CompilerParams(
            collective_id=0, has_side_effects=True, vmem_limit_bytes=61730 * 1024
        ),
        name="eigen",
    )(lengths, grads.reshape(2, tokens // 2, width), acts, out_basis, in_basis)


def solution(mesh):
    in_specs = (
        P("row", ("seq", "col")),
        P(("seq", "col"), "row"),
        P(("seq", "col"), "row"),
        P("row", ("seq", "col")),
        P(),
    )
    out_specs = P("row", ("seq", "col"))
    return jax.shard_map(body, mesh=mesh, in_specs=in_specs, out_specs=out_specs, check_vma=False)
```
